32 devices in a mesh: section: 2 (over core), band: 16 (over z, y, x).
Axes of the slice: x: 2, y: 2, z: 4, core: 2. Of those that a mesh axis runs over, the one named last changes fastest.
Arguments:
- image: bfloat16 [32, 160, 320], P('band'), may hold values from -6 to 6
- carried: bfloat16 [2, 32, 160, 320], P('section', 'band'), may hold values from -6 to 6
- saved: bfloat16 [2, 32, 160, 320], P('section', 'band'), may hold values from -6 to 6
- sent_grad: bfloat16 [2, 32, 160, 320], P('section', 'band'), may hold values from -6 to 6
- loss_grad: bfloat16 [32, 160, 320], P('band'), may hold values from -6 to 6
- first_kernel: bfloat16 [2, 2880, 320], P('section'), may hold values from -0.109375 to 0.109375
- second_kernel: bfloat16 [2, 2880, 320], P('section'), may hold values from -0.109375 to 0.109375
Outputs:
- forward_out: bfloat16 [2, 32, 160, 320], P('section', 'band')
- input_grad: bfloat16 [2, 32, 160, 320], P('section', 'band')
- first_kernel_grad: float32 [2, 2880, 320], P('section', 'band')
- second_kernel_grad: float32 [2, 2880, 320], P('section', 'band')
The draws below stay inside these ranges and needn't reach their ends.
All inputs are finite; a program needn't handle non-finite values.
Results may differ from the reference program's by a relative error of at most 0.0033.
Values may be sent and summed in bfloat16 or wider, within the bound.
No kernel may reach another device: no remote copies, remote signals or barrier semaphores. Data moves between devices by JAX's collectives and lax.ppermute only.
A program may use at most 128 MiB of HBM per device.

```python
import jax
import jax.numpy as jnp
from jax import lax

C = 320
COLS = 160
SECTIONS = 2
NROWS = 32


def shard_levels(own_key, dims, shards, least, high):
    level = 1.0
    for position, blocks in shards:
        draws = jax.random.uniform(jax.random.fold_in(jax.random.fold_in(own_key, 6), position), (blocks,), jnp.float32, least / len(shards), high / len(shards))
        level = level * jnp.repeat(jnp.exp(draws), dims[position] // blocks).reshape((-1,) + (1,) * (len(dims) - 1 - position))
    return level


def bell_draw(stream_key, extent, deviation, limit, cuts=(), held_as=jnp.bfloat16):
    factor_of = shard_levels(stream_key, extent, cuts, -0.22, 0.18) if cuts else 1.0
    drawn = jax.random.normal(stream_key, extent, jnp.float32) * deviation * factor_of
    return jnp.minimum(jnp.maximum(drawn, -limit), limit).astype(held_as)


def setup_inputs(seed: int = 0) -> dict:
    keys = jax.random.split(jax.random.key(seed), 8)
    return {
        "image": bell_draw(keys[0], (NROWS, COLS, C), 1.0, 6.0, ((0, 16),)),
        "carried": bell_draw(keys[1], (SECTIONS, NROWS, COLS, C), 1.0, 6.0, ((0, 2), (1, 16))),
        "saved": bell_draw(keys[2], (SECTIONS, NROWS, COLS, C), 1.0, 6.0, ((0, 2), (1, 16))),
        "sent_grad": bell_draw(keys[3], (SECTIONS, NROWS, COLS, C), 1.0, 6.0, ((0, 2), (1, 16))),
        "loss_grad": bell_draw(keys[4], (NROWS, COLS, C), 1.0, 6.0, ((0, 16),)),
        "first_kernel": bell_draw(keys[5], (SECTIONS, 9 * C, C), (9 * C) ** -0.5, 0.109375, ((0, 2),)),
        "second_kernel": bell_draw(keys[6], (SECTIONS, 9 * C, C), (9 * C) ** -0.5, 0.109375, ((0, 2),)),
    }


def convolve(padded, kernel, height, breadth):
    taps = kernel.reshape(9, kernel.shape[0] // 9, kernel.shape[1])
    total = jnp.zeros((height * breadth, kernel.shape[1]), jnp.float32)
    for tapnum in range(9):
        row_off, col_off = divmod(tapnum, 3)
        piece = padded[row_off:row_off + height, col_off:col_off + breadth].reshape(height * breadth, -1)
        total = total + jnp.dot(piece, taps[tapnum], preferred_element_type=jnp.float32)
    return total.reshape(height, breadth, -1)


def convolve_back(padded, kernel, height, breadth):
    taps = kernel.reshape(9, kernel.shape[0] // 9, kernel.shape[1])
    total = jnp.zeros((height * breadth, kernel.shape[0] // 9), jnp.float32)
    for tapnum in range(9):
        row_off, col_off = divmod(tapnum, 3)
        piece = padded[2 - row_off:2 - row_off + height, 2 - col_off:2 - col_off + breadth].reshape(height * breadth, -1)
        total = total + jnp.dot(piece, taps[tapnum].T, preferred_element_type=jnp.float32)
    return total.reshape(height, breadth, -1)


def kernel_terms(values, padded, height, breadth):
    flat = values.reshape(height * breadth, -1)
    blocks = []
    for tapnum in range(9):
        row_off, col_off = divmod(tapnum, 3)
        piece = padded[2 - row_off:2 - row_off + height, 2 - col_off:2 - col_off + breadth].reshape(height * breadth, -1)
        blocks.append(lax.dot_general(flat, piece, (((0,), (0,)), ((), ())), preferred_element_type=jnp.float32))
    return jnp.concatenate(blocks, axis=0)


def silu_slope(preact):
    sig = jax.nn.sigmoid(preact)
    return sig * (1.0 + preact * (1.0 - sig))


def pad_all(values):
    return jnp.pad(values, ((1, 1), (1, 1), (0, 0)))


def one_section(operands):
    x_in, stored, g_in, first, second = operands
    preact = convolve(pad_all(x_in), first, NROWS, COLS)
    act = jax.nn.silu(preact).astype(jnp.bfloat16)
    forward_out = (x_in.astype(jnp.float32) + convolve(pad_all(act), second, NROWS, COLS)).astype(jnp.bfloat16)
    pre_back = convolve(pad_all(stored), first, NROWS, COLS)
    act_back = jax.nn.silu(pre_back).astype(jnp.bfloat16)
    grad_padded = pad_all(g_in)
    grad_act = convolve_back(grad_padded, second, NROWS, COLS)
    grad_pre = (grad_act * silu_slope(pre_back)).astype(jnp.bfloat16)
    inner_padded = pad_all(grad_pre)
    input_grad = (g_in.astype(jnp.float32) + convolve_back(inner_padded, first, NROWS, COLS)).astype(jnp.bfloat16)
    factor = (NROWS * COLS) ** -0.5
    first_grad = kernel_terms(stored, inner_padded, NROWS, COLS) * factor
    second_grad = kernel_terms(act_back, grad_padded, NROWS, COLS) * factor
    return forward_out, input_grad, first_grad, second_grad


def reference(image, carried, saved, sent_grad, loss_grad, first_kernel, second_kernel):
    inputs = jnp.concatenate([image[None], carried[:-1]], axis=0)
    grads_in = jnp.concatenate([sent_grad[1:], loss_grad[None]], axis=0)
    forward_out, input_grad, first_grad, second_grad = lax.map(one_section, (inputs, saved, grads_in, first_kernel, second_kernel))
    return forward_out, input_grad, first_grad, second_grad
```

```python
import functools
import math

import jax
import jax.numpy as jnp
from jax import lax
from jax.experimental import pallas as pl
from jax.experimental.pallas import tpu as pltpu
from jax.sharding import PartitionSpec as P

F32 = jnp.float32
BF16 = jnp.bfloat16
VMEM = pltpu.VMEM


def call(kernel, outs, scratch=(), name=None):
    def run(*args):
        return pl.pallas_call(
            kernel,
            out_shape=outs,
            in_specs=[pl.BlockSpec(memory_space=VMEM)] * len(args),
            out_specs=jax.tree.map(lambda _: pl.BlockSpec(memory_space=VMEM), outs),
            scratch_shapes=scratch,
            name=name,
        )(*args)

    return run


def put_row(cat, row, value):
    cols, chans = value.shape
    wide = value.astype(F32)
    place = lax.broadcasted_iota(jnp.int32, (cols, chans), 0)
    left = jnp.where(place == 0, 0.0, pltpu.roll(wide, 1, 0)).astype(BF16)
    right = jnp.where(place == cols - 1, 0.0, pltpu.roll(wide, cols - 1, 0)).astype(BF16)
    at = pl.ds(pl.multiple_of(row * cols, cols), cols)
    cat[at, 0:chans] = left
    cat[at, chans : 2 * chans] = value
    cat[at, 2 * chans : 3 * chans] = right


def conv_rows(cat, kernel, start, rows, cols):
    deep = kernel.shape[0] // 3
    total = None
    for dy in range(3):
        at = start + dy
        at = at * cols if isinstance(at, int) else pl.multiple_of(at * cols, cols)
        part = jnp.dot(
            cat[pl.ds(at, rows * cols), :],
            kernel[dy * deep : (dy + 1) * deep, :],
            preferred_element_type=F32,
        )
        total = part if total is None else total + part
    return total


def turn_kernel(first, second, first_t, second_t):
    chans = first.shape[1]
    for src, dst in ((second, second_t), (first, first_t)):
        for tap in range(9):
            dst[tap * chans : (tap + 1) * chans, :] = src[
                (8 - tap) * chans : (9 - tap) * chans, :
            ].T


def place_of(rel, masks):
    top = max(masks).bit_length() - 1
    bits = [(rel >> i) & 1 for i in range(top + 1)]
    pos = 0
    for m in masks:
        if m & (m - 1):
            a = bits[top]
        elif m.bit_length() - 1 == top - 1:
            a = bits[top - 1] ^ bits[top]
        else:
            a = bits[m.bit_length() - 1]
        pos = pos * 2 + a
    return pos


def store_terms(terms, base, value, band, bands, masks):
    share = terms.share
    rows = value.shape[0]
    for block in range(bands):
        lo, hi = max(base, block * share), min(base + rows, (block + 1) * share)
        if lo >= hi:
            continue
        off = lo - block * share + (block * share) % 8
        pos = place_of((block ^ band) >> 1, masks)

        @pl.when((band & 1) == (block & 1))
        def _(lo=lo, hi=hi, off=off, pos=pos):
            terms.ref[pos, off : off + hi - lo, :] = value[lo - base : hi - base, :]


class Terms:
    def __init__(self, ref, share):
        self.ref = ref
        self.share = share


def finish_terms(terms, keep, send):
    half = keep.shape[0]
    for i in range(half):
        keep[i] = terms[i]
        send[i] = terms[half + i].astype(BF16)


def load_slab(cat, own, par, near, far, index, side, rows):
    for r in range(rows):
        put_row(cat, 1 + rows * side + r, own[r])
        put_row(cat, 1 + rows * (1 - side) + r, par[r])
    put_row(cat, (1 - side) * (2 * rows + 1), near[index])
    put_row(cat, side * (2 * rows + 1), far[index])


def back_one(bands, masks, share, own, par, g_own, g_par, near, far, kernel, slope, scat, gcat, keep, send, terms):
    rows, cols, chans = own.shape
    band = lax.axis_index("band")
    side = band & 1
    load_slab(scat, own, par, near, far, 0, side, rows)
    load_slab(gcat, g_own, g_par, near, far, 1, side, rows)
    pre = conv_rows(scat, kernel, 0, 2 * rows, cols)
    sig = jax.nn.sigmoid(pre)
    act = (pre * sig).astype(BF16)
    slope[...] = sig * (1.0 + pre * (1.0 - sig))
    held = Terms(terms, share)
    turned = act.T
    for ky in range(3):
        block = gcat[(2 - ky) * cols : (2 - ky + 2 * rows) * cols, :]
        out = jnp.dot(turned, block, preferred_element_type=F32)
        for kx in range(3):
            store_terms(
                held,
                (3 * ky + kx) * chans,
                out[:, (2 - kx) * chans : (3 - kx) * chans],
                band,
                bands,
                masks,
            )
    finish_terms(terms, keep, send)


def back_two(bands, masks, share, gcat, scat, slope, kernel_t, inner, keep, send, terms):
    rows2, cols, chans = inner.shape
    band = lax.axis_index("band")
    grad = (conv_rows(gcat, kernel_t, 0, rows2, cols) * slope[...]).astype(BF16)
    inner[...] = grad.reshape(rows2, cols, chans)
    held = Terms(terms, share)
    for ky in range(3):
        out = lax.dot_general(
            scat[ky * cols : (ky + rows2) * cols, :],
            grad,
            (((0,), (0,)), ((), ())),
            preferred_element_type=F32,
        )
        store_terms(held, 3 * ky * chans, out, band, bands, masks)
    finish_terms(terms, keep, send)


def ahead_one(own, par, far, kernel, act, cat):
    rows, cols, chans = own.shape
    side = lax.axis_index("band") & 1
    for r in range(rows):
        put_row(cat, 1 + rows * side + r, own[r])
        put_row(cat, 1 + rows * (1 - side) + r, par[r])
    put_row(cat, side * (2 * rows + 1), far[0])
    start = side * (rows - 1)
    pre = conv_rows(cat, kernel, start, rows + 1, cols)
    act[...] = (pre * jax.nn.sigmoid(pre)).astype(BF16).reshape(act.shape)


def last_conv(offset, inner, edge, kernel, base, out, cat):
    rows, cols, chans = base.shape
    side = lax.axis_index("band") & 1
    for r in range(rows + 1):
        put_row(cat, 1 - side + r, inner[offset * side * (rows - 1) + r])
    put_row(cat, side * (rows + 1), edge[0])
    total = conv_rows(cat, kernel, 0, rows, cols)
    out[...] = (base[...].astype(F32) + total.reshape(rows, cols, chans)).astype(BF16)


def body(image, carried, saved, sent_grad, loss_grad, first_kernel, second_kernel):
    rows, cols, chans = image.shape
    first, second, stored = first_kernel[0], second_kernel[0], saved[0]
    bands = lax.axis_size("band")
    sections = lax.axis_size("section")
    band = lax.axis_index("band")
    section = lax.axis_index("section")
    side = band & 1
    share = first.shape[0] // bands
    pitch = -(-(share + max(b * share % 8 for b in range(bands))) // 8) * 8
    half = bands // 2

    partner = [(b, b ^ 1) for b in range(bands)]
    beyond = [(b, b + 2 * (2 * (b & 1) - 1)) for b in range(bands)]
    beyond = [(a, b) for a, b in beyond if 0 <= b < bands]
    across = [(b, b + 2 * (b & 1) - 1) for b in range(bands)]
    across = [(a, b) for a, b in across if 0 <= b < bands]

    stored_par = lax.ppermute(stored, "band", partner)
    if sections == 2:
        gone = jnp.where(section == 0, carried[0], sent_grad[0])
        got = lax.ppermute(gone, "section", [(0, 1), (1, 0)])
        arrived = returned = got
    else:
        up = [(i, i + 1) for i in range(sections - 1)]
        arrived = lax.ppermute(carried[0], "section", up)
        returned = lax.ppermute(sent_grad[0], "section", [(b, a) for a, b in up])
    x_in = jnp.where(section == 0, image, arrived)
    g_in = jnp.where(section == sections - 1, loss_grad, returned)

    def edge(value):
        return lax.dynamic_slice_in_dim(value, side * (rows - 1), 1, axis=0)

    near = lax.ppermute(jnp.concatenate([edge(stored), edge(g_in)], axis=0), "band", beyond)
    g_par = lax.ppermute(g_in, "band", partner)
    far = lax.ppermute(near, "band", partner)
    x_par = lax.ppermute(x_in, "band", partner)
    x_far = lax.ppermute(edge(x_in), "band", across)

    first_t, second_t = call(
        turn_kernel,
        [jax.ShapeDtypeStruct(first.shape, BF16)] * 2,
        name="turn",
    )(first, second)

    bits = bands.bit_length() - 2
    singles = [1 << i for i in range(bits - 1)]
    last = 3 << (bits - 2)
    orders = (singles + [last], singles[::-1] + [last])

    pixels = 2 * rows * cols
    cat_shape = jax.ShapeDtypeStruct(((2 * rows + 2) * cols, 3 * chans), BF16)
    keep_shape = jax.ShapeDtypeStruct((half // 2, pitch, chans), F32)
    send_shape = jax.ShapeDtypeStruct((half // 2, pitch, chans), BF16)
    terms = pltpu.VMEM((half, pitch, chans), F32)

    slope, scat, gcat, keep2, send2 = call(
        functools.partial(back_one, bands, orders[0], share),
        [jax.ShapeDtypeStruct((pixels, chans), F32), cat_shape, cat_shape, keep_shape, send_shape],
        [terms],
        name="back_one",
    )(stored, stored_par, g_in, g_par, near, far, first)
    inner, keep1, send1 = call(
        functools.partial(back_two, bands, orders[1], share),
        [jax.ShapeDtypeStruct((2 * rows, cols, chans), BF16), keep_shape, send_shape],
        [terms],
        name="back_two",
    )(gcat, scat, slope, second_t)

    def scatter(keep, send, masks):
        for mask in masks:
            pairs = [(b, b ^ (mask << 1)) for b in range(bands)]
            got = lax.ppermute(send, "band", pairs)
            now = keep.shape[0] // 2
            if now:
                send = (keep[now:] + got[now:].astype(F32)).astype(BF16)
                keep = keep[:now] + got[:now].astype(F32)
            else:
                keep = keep + got.astype(F32)
        off = (band * share) % 8
        return lax.dynamic_slice_in_dim(keep[0], off, share, axis=0)

    second_sum = scatter(keep2, send2, orders[0])
    first_sum = scatter(keep1, send1, orders[1])

    small_cat = pltpu.VMEM(((rows + 2) * cols, 3 * chans), BF16)
    act = call(
        ahead_one,
        jax.ShapeDtypeStruct((rows + 1, cols, chans), BF16),
        [pltpu.VMEM(cat_shape.shape, BF16)],
        name="ahead_one",
    )(x_in, x_par, x_far, first)
    act_edge = lax.ppermute(
        lax.dynamic_slice_in_dim(act, side * rows, 1, axis=0), "band", across
    )
    inner_edge = lax.ppermute(
        lax.dynamic_slice_in_dim(inner, side * (2 * rows - 1), 1, axis=0), "band", across
    )
    forward_out = call(
        functools.partial(last_conv, 0),
        jax.ShapeDtypeStruct(x_in.shape, BF16),
        [small_cat],
        name="ahead_two",
    )(act, act_edge, second, x_in)
    input_grad = call(
        functools.partial(last_conv, 1),
        jax.ShapeDtypeStruct(g_in.shape, BF16),
        [small_cat],
        name="back_three",
    )(inner, inner_edge, first_t, g_in)
    factor = 1.0 / math.sqrt(rows * bands * cols)
    return (
        forward_out[None],
        input_grad[None],
        (first_sum * factor)[None],
        (second_sum * factor)[None],
    )


def solution(mesh):
    return jax.shard_map(
        body,
        mesh=mesh,
        in_specs=(
            P("band", None, None),
            P("section", "band", None, None),
            P("section", "band", None, None),
            P("section", "band", None, None),
            P("band", None, None),
            P("section", None, None),
            P("section", None, None),
        ),
        out_specs=(
            P("section", "band", None, None),
            P("section", "band", None, None),
            P("section", "band", None),
            P("section", "band", None),
        ),
        check_vma=False,
    )
```

```python
import functools
import math

import jax
import jax.numpy as jnp
from jax import lax
from jax.experimental import pallas as pl
from jax.experimental.pallas import tpu as pltpu
from jax.sharding import PartitionSpec as P


F32 = jnp.float32
BF16 = jnp.bfloat16
VMEM = pltpu.VMEM


def call(kernel, outs, scratch=(), limit=20, space=VMEM):
    def kernel_call(*args):
        return pl.pallas_call(
            kernel,
            out_shape=outs,
            in_specs=[pl.BlockSpec(memory_space=space)] * len(args),
            out_specs=jax.tree.map(lambda _: pl.BlockSpec(memory_space=VMEM), outs),
            scratch_shapes=scratch,
            compiler_params=pltpu.CompilerParams(vmem_limit_bytes=limit << 20),
        )(*args)

    return kernel_call


def put_row(cat, row, value):
    cols, chans = value.shape
    wide = value.astype(F32)
    value = value.astype(BF16)
    place = lax.broadcasted_iota(jnp.int32, (cols, chans), 0)
    left = jnp.where(place == 0, 0.0, pltpu.roll(wide, 1, 0)).astype(BF16)
    right = jnp.where(place == cols - 1, 0.0, pltpu.roll(wide, cols - 1, 0)).astype(BF16)
    at = pl.ds(pl.multiple_of(row * cols, cols), cols)
    cat[at, 0:chans] = left
    cat[at, chans : 2 * chans] = value
    cat[at, 2 * chans : 3 * chans] = right


def conv_rows(cat, kernel, start, rows, cols):
    deep = kernel.shape[0] // 3
    total = None
    for dy in range(3):
        at = start + dy
        at = at * cols if isinstance(at, int) else pl.multiple_of(at * cols, cols)
        part = jnp.dot(
            cat[pl.ds(at, rows * cols), :],
            kernel[dy * deep : (dy + 1) * deep, :],
            preferred_element_type=F32,
        )
        total = part if total is None else total + part
    return total


LANES = 128


def packed_len(count, chans):
    return count * (chans // LANES) + count // 2 * (1 if chans % LANES else 0)


def pack_pair(out, at, low, high):
    chans = low.shape[1]
    whole = chans // LANES
    for part, value in enumerate((low, high)):
        for i in range(whole):
            out[at + part * whole + i] = value[:, i * LANES : (i + 1) * LANES].astype(BF16)
    if chans % LANES:
        rest = jnp.concatenate([low[:, whole * LANES :], high[:, whole * LANES :]], axis=1)
        out[at + 2 * whole] = rest.astype(BF16)


def unpack_pair(src, at, chans):
    whole = chans // LANES
    both = []
    for part in range(2):
        pieces = [src[at + part * whole + i].astype(F32) for i in range(whole)]
        wide = chans - whole * LANES
        if wide:
            rest = src[at + 2 * whole].astype(F32)
            pieces.append(rest[:, part * wide : (part + 1) * wide])
        both.append(jnp.concatenate(pieces, axis=1))
    return both


def begin_kernel(
    carried, sent_grad, stored, image, loss_grad, gone, stored_in, image_in, loss_in, stored_out, sems
):
    rows, _, chans = stored.shape
    section = lax.axis_index("section")
    first = pltpu.make_async_copy(carried, gone, sems.at[0])
    other = pltpu.make_async_copy(sent_grad, gone, sems.at[0])
    pl.when(section == 0)(first.start)
    pl.when(section != 0)(other.start)
    copies = [
        pltpu.make_async_copy(src, dst, sems.at[1 + i])
        for i, (src, dst) in enumerate(
            ((stored, stored_in), (image, image_in), (loss_grad, loss_in))
        )
    ]
    for copy in copies:
        copy.start()
    copies[0].wait()
    step = packed_len(2, chans)
    for r in range(0, rows, 2):
        pack_pair(
            stored_out, r // 2 * step, stored_in[r].astype(F32), stored_in[r + 1].astype(F32)
        )
    for copy in copies[1:]:
        copy.wait()
    pl.when(section == 0)(first.wait)
    pl.when(section != 0)(other.wait)


def middle_kernel(
    sections, arrived, returned, image, loss_grad, stored, x_in, g_in, x_out, g_out, edges, x_edge
):
    rows, _, chans = image.shape
    section = lax.axis_index("section")
    side = lax.axis_index("band") & 1

    @pl.when(section == 0)
    def _():
        x_in[...] = image[...]

    @pl.when(section != 0)
    def _():
        x_in[...] = arrived[...]

    @pl.when(section == sections - 1)
    def _():
        g_in[...] = loss_grad[...]

    @pl.when(section != sections - 1)
    def _():
        g_in[...] = returned[...]

    row = side * (rows - 1)
    pack_pair(edges, 0, stored[row].astype(F32), g_in[row].astype(F32))
    x_edge[0] = x_in[row]
    step = packed_len(2, chans)
    for r in range(0, rows, 2):
        pack_pair(g_out, r // 2 * step, g_in[r].astype(F32), g_in[r + 1].astype(F32))
        pack_pair(x_out, r // 2 * step, x_in[r].astype(F32), x_in[r + 1].astype(F32))


def turn_kernel(kernel_t, kernel, back):
    chans = kernel.shape[1]
    for tap in range(9):
        block = kernel_t[:, tap * chans : (tap + 1) * chans]
        kernel[tap * chans : (tap + 1) * chans, :] = block.T
        back[(8 - tap) * chans : (9 - tap) * chans, :] = block


def place_of(rel, masks):
    top = max(masks).bit_length() - 1
    bits = [(rel >> i) & 1 for i in range(top + 1)]
    pos = 0
    for m in masks:
        if m & (m - 1):
            a = bits[top]
        elif m.bit_length() - 1 == top - 1:
            a = bits[top - 1] ^ bits[top]
        else:
            a = bits[m.bit_length() - 1]
        pos = pos * 2 + a
    return pos


def store_terms(terms, base, value, band, bands, masks):
    share = terms.share
    rows = value.shape[0]
    for block in range(bands):
        lo, hi = max(base, block * share), min(base + rows, (block + 1) * share)
        if lo >= hi:
            continue
        off = lo - block * share + (block * share) % 8
        pos = place_of((block ^ band) >> 1, masks)

        @pl.when((band & 1) == (block & 1))
        def _(lo=lo, hi=hi, off=off, pos=pos):
            terms.ref[pos, off : off + hi - lo, :] = value[lo - base : hi - base, :]


class Terms:
    def __init__(self, ref, share):
        self.ref = ref
        self.share = share


def send_blocks(send, blocks):
    if len(blocks) == 1:
        send[0] = blocks[0].astype(BF16)
        return
    step = packed_len(2, blocks[0].shape[1])
    for i in range(0, len(blocks), 2):
        pack_pair(send, i // 2 * step, blocks[i], blocks[i + 1])


def finish_terms(terms, keep, send):
    half = keep.shape[0]
    for i in range(half):
        keep[i] = terms[i]
    send_blocks(send, [terms[half + i] for i in range(half)])


def merge_kernel(keep, got, keep_out, send_out):
    count, _, chans = keep.shape
    step = packed_len(2, chans)
    total = []
    for i in range(0, count, 2):
        low, high = unpack_pair(got, i // 2 * step, chans)
        total += [keep[i] + low, keep[i + 1] + high]
    for i in range(count // 2):
        keep_out[i] = total[i]
    send_blocks(send_out, total[count // 2 :])


def last_sum(bands, factor, keep, got, out):
    share, _, chans = out.shape
    band = lax.axis_index("band")
    starts = {b * share % 8 for b in range(bands)}
    for start in sorted(starts):

        @pl.when(lax.rem(band * share, 8) == start)
        def _(start=start):
            rows = slice(start, start + share)
            total = (keep[0, rows, :] + got[0, rows, :].astype(F32)) * factor
            out[...] = total.reshape(share, 1, chans)


def load_rows(cat, own, par, side):
    rows, _, chans = own.shape
    step = packed_len(2, chans)
    for r in range(0, rows, 2):
        pair = unpack_pair(par, r // 2 * step, chans)
        for i in range(2):
            put_row(cat, 1 + rows * side + r + i, own[r + i])
            put_row(cat, 1 + rows * (1 - side) + r + i, pair[i])


def load_slab(cat, own, par, near, far, index, side):
    rows, _, chans = own.shape
    load_rows(cat, own, par, side)
    put_row(cat, (1 - side) * (2 * rows + 1), unpack_pair(near, 0, chans)[index])
    put_row(cat, side * (2 * rows + 1), unpack_pair(far, 0, chans)[index])


def back_pre(own, par, near, far, kernel, turned, slope, cat):
    rows, cols, _ = own.shape
    load_slab(cat, own, par, near, far, 0, lax.axis_index("band") & 1)
    pre = conv_rows(cat, kernel, 0, 2 * rows, cols)
    sig = jax.nn.sigmoid(pre)
    turned[...] = (pre * sig).astype(BF16).T
    slope[...] = sig * (1.0 + pre * (1.0 - sig))


def back_one(bands, masks, share, own, par, near, far, turned, cat, keep, send, terms):
    rows, cols, chans = own.shape
    band = lax.axis_index("band")
    load_slab(cat, own, par, near, far, 1, band & 1)
    held = Terms(terms, share)
    for ky in range(3):
        block = cat[(2 - ky) * cols : (2 - ky + 2 * rows) * cols, :]
        out = jnp.dot(turned[...], block, preferred_element_type=F32)
        for kx in range(3):
            store_terms(
                held,
                (3 * ky + kx) * chans,
                out[:, (2 - kx) * chans : (3 - kx) * chans],
                band,
                bands,
                masks,
            )
    finish_terms(terms, keep, send)


def back_two(
    bands, masks, share, gcat, scat, slope, kernel_t, inner, edge, keep, send, terms
):
    rows2, cols, chans = inner.shape
    band = lax.axis_index("band")
    grad = (conv_rows(gcat, kernel_t, 0, rows2, cols) * slope[...]).astype(BF16)
    inner[...] = grad.reshape(rows2, cols, chans)
    edge[0] = inner[(band & 1) * (rows2 - 1)]
    held = Terms(terms, share)
    for ky in range(3):
        out = lax.dot_general(
            scat[ky * cols : (ky + rows2) * cols, :],
            grad,
            (((0,), (0,)), ((), ())),
            preferred_element_type=F32,
        )
        store_terms(held, 3 * ky * chans, out, band, bands, masks)
    finish_terms(terms, keep, send)


def ahead_one(own, par, far, kernel, act, edge, cat):
    rows, cols, _ = own.shape
    side = lax.axis_index("band") & 1
    load_rows(cat, own, par, side)
    put_row(cat, side * (2 * rows + 1), far[0])
    start = side * (rows - 1)
    pre = conv_rows(cat, kernel, start, rows + 1, cols)
    act[...] = (pre * jax.nn.sigmoid(pre)).astype(BF16).reshape(act.shape)
    edge[0] = act[side * rows]


def last_conv(offset, inner, edge, kernel, base, out, cat):
    rows, cols, chans = base.shape
    side = lax.axis_index("band") & 1
    for r in range(rows + 1):
        put_row(cat, 1 - side + r, inner[offset * side * (rows - 1) + r])
    put_row(cat, side * (rows + 1), edge[0])
    total = conv_rows(cat, kernel, 0, rows, cols)
    out[...] = (base[...].astype(F32) + total.reshape(rows, cols, chans)).astype(BF16)


def body(image, carried, saved, sent_grad, loss_grad, first_kernel, second_kernel):
    rows, cols, chans = image.shape
    first, second = first_kernel[0], second_kernel[0]
    bands = lax.axis_size("band")
    sections = lax.axis_size("section")
    share = first.shape[0] // bands
    pitch = -(-(share + max(b * share % 8 for b in range(bands))) // 8) * 8
    half = bands // 2

    partner = [(b, b ^ 1) for b in range(bands)]
    beyond = [(b, b + 2 * (2 * (b & 1) - 1)) for b in range(bands)]
    beyond = [(a, b) for a, b in beyond if 0 <= b < bands]
    across = [(b, b + 2 * (b & 1) - 1) for b in range(bands)]
    across = [(a, b) for a, b in across if 0 <= b < bands]

    def move(value, pairs, axis="band"):
        return lax.ppermute(value, axis, pairs)

    whole_shape = jax.ShapeDtypeStruct(image.shape, BF16)
    row_shape = jax.ShapeDtypeStruct((1, cols, chans), BF16)

    def packed(count, rows=cols):
        return jax.ShapeDtypeStruct((packed_len(count, chans), rows, LANES), BF16)

    gone, stored, image, loss_grad, stored_out = call(
        begin_kernel,
        [whole_shape] * 4 + [packed(rows)],
        [pltpu.SemaphoreType.DMA((4,))],
        space=pltpu.HBM,
    )(*(
        pltpu.with_memory_space_constraint(v, pltpu.HBM)
        for v in (carried[0], sent_grad[0], saved[0], image, loss_grad)
    ))
    if sections == 2:
        arrived = returned = move(gone, [(0, 1), (1, 0)], "section")
    else:
        up = [(i, i + 1) for i in range(sections - 1)]
        returned = move(sent_grad[0], [(b, a) for a, b in up], "section")
        arrived = move(carried[0], up, "section")
    stored_par = move(stored_out, partner)
    x_in, g_in, x_out, g_out, edges, x_edge = call(
        functools.partial(middle_kernel, sections),
        [whole_shape, whole_shape, packed(rows), packed(rows), packed(2), row_shape],
    )(arrived, returned, image, loss_grad, stored)
    near = move(edges, beyond)
    far = move(edges, across)
    g_par = move(g_out, partner)
    x_par = move(x_out, partner)
    x_far = move(x_edge, across)

    turned_shapes = [jax.ShapeDtypeStruct(first.shape, BF16)] * 2
    first_k, first_t = call(turn_kernel, turned_shapes)(first.T)
    second_k, second_t = call(turn_kernel, turned_shapes)(second.T)

    bits = bands.bit_length() - 2
    singles = [1 << i for i in range(bits - 1)]
    last = 3 << (bits - 2)
    orders = (singles + [last], singles[::-1] + [last])

    pixels = 2 * rows * cols
    cat_shape = jax.ShapeDtypeStruct(((2 * rows + 2) * cols, 3 * chans), BF16)
    keep_shape = jax.ShapeDtypeStruct((half // 2, pitch, chans), F32)

    def send_of(count):
        if count == 1:
            return jax.ShapeDtypeStruct((1, pitch, chans), BF16)
        return packed(count, pitch)

    send_shape = send_of(half // 2)
    terms = pltpu.VMEM((half, pitch, chans), F32)

    turned, slope, scat = call(
        back_pre,
        [
            jax.ShapeDtypeStruct((chans, pixels), BF16),
            jax.ShapeDtypeStruct((pixels, chans), F32),
            cat_shape,
        ],
    )(stored, stored_par, near, far, first_k)
    gcat, keep2, send2 = call(
        functools.partial(back_one, bands, orders[0], share),
        [cat_shape, keep_shape, send_shape],
        [terms],
    )(g_in, g_par, near, far, turned)
    inner, inner_edge, keep1, send1 = call(
        functools.partial(back_two, bands, orders[1], share),
        [jax.ShapeDtypeStruct((2 * rows, cols, chans), BF16), row_shape, keep_shape, send_shape],
        [terms],
    )(gcat, scat, slope, second_t)

    factor = 1.0 / math.sqrt(rows * bands * cols)

    def scatter(keep, send, masks):
        for mask in masks:
            pairs = [(b, b ^ (mask << 1)) for b in range(bands)]
            got = move(send, pairs)
            now = keep.shape[0] // 2
            if now:
                keep, send = call(
                    merge_kernel,
                    [jax.ShapeDtypeStruct((now, pitch, chans), F32), send_of(now)],
                )(keep, got)
        return call(
            functools.partial(last_sum, bands, factor),
            jax.ShapeDtypeStruct((share, 1, chans), F32),
        )(keep, got).reshape(1, share, chans)

    second_sum = scatter(keep2, send2, orders[0])
    first_sum = scatter(keep1, send1, orders[1])

    small_cat = pltpu.VMEM(((rows + 2) * cols, 3 * chans), BF16)
    act, act_edge = call(
        ahead_one,
        [jax.ShapeDtypeStruct((rows + 1, cols, chans), BF16), row_shape],
        [pltpu.VMEM(cat_shape.shape, BF16)],
    )(x_in, x_par, x_far, first_k)
    act_edge = move(act_edge, across)
    inner_edge = move(inner_edge, across)
    forward_out = call(
        functools.partial(last_conv, 0),
        jax.ShapeDtypeStruct(x_in.shape, BF16),
        [small_cat],
    )(act, act_edge, second_k, x_in)
    input_grad = call(
        functools.partial(last_conv, 1),
        jax.ShapeDtypeStruct(g_in.shape, BF16),
        [small_cat],
    )(inner, inner_edge, first_t, g_in)
    return (
        forward_out[None],
        input_grad[None],
        first_sum,
        second_sum,
    )


def solution(mesh):
    return jax.shard_map(
        body,
        mesh=mesh,
        in_specs=(
            P("band", None, None),
            P("section", "band", None, None),
            P("section", "band", None, None),
            P("section", "band", None, None),
            P("band", None, None),
            P("section", None, None),
            P("section", None, None),
        ),
        out_specs=(
            P("section", "band", None, None),
            P("section", "band", None, None),
            P("section", "band", None),
            P("section", "band", None),
        ),
        check_vma=False,
    )
```

```python
import functools
import math

import jax
import jax.numpy as jnp
from jax import lax
from jax.experimental import pallas as pl
from jax.experimental.pallas import tpu as pltpu
from jax.sharding import PartitionSpec as P


F32 = jnp.float32
BF16 = jnp.bfloat16
VMEM = pltpu.VMEM


def call(kernel, outs, scratch=(), limit=20, space=VMEM):
    def kernel_call(*args):
        return pl.pallas_call(
            kernel,
            out_shape=outs,
            in_specs=[pl.BlockSpec(memory_space=space)] * len(args),
            out_specs=jax.tree.map(lambda _: pl.BlockSpec(memory_space=VMEM), outs),
            scratch_shapes=scratch,
            compiler_params=pltpu.CompilerParams(vmem_limit_bytes=limit << 20),
        )(*args)

    return kernel_call


def put_row(cat, row, value):
    cols, chans = value.shape
    wide = value.astype(F32)
    value = value.astype(BF16)
    place = lax.broadcasted_iota(jnp.int32, (cols, chans), 0)
    left = jnp.where(place == 0, 0.0, pltpu.roll(wide, 1, 0)).astype(BF16)
    right = jnp.where(place == cols - 1, 0.0, pltpu.roll(wide, cols - 1, 0)).astype(BF16)
    at = pl.ds(pl.multiple_of(row * cols, cols), cols)
    cat[at, 0:chans] = left
    cat[at, chans : 2 * chans] = value
    cat[at, 2 * chans : 3 * chans] = right


def conv_rows(cat, kernel, start, rows, cols):
    deep = kernel.shape[0] // 3
    total = None
    for dy in range(3):
        at = start + dy
        at = at * cols if isinstance(at, int) else pl.multiple_of(at * cols, cols)
        part = jnp.dot(
            cat[pl.ds(at, rows * cols), :],
            kernel[dy * deep : (dy + 1) * deep, :],
            preferred_element_type=F32,
        )
        total = part if total is None else total + part
    return total


LANES = 128


def packed_len(count, chans):
    return count * (chans // LANES) + count // 2 * (1 if chans % LANES else 0)


def pack_pair(out, at, low, high):
    chans = low.shape[1]
    whole = chans // LANES
    for part, value in enumerate((low, high)):
        for i in range(whole):
            out[at + part * whole + i] = value[:, i * LANES : (i + 1) * LANES].astype(BF16)
    if chans % LANES:
        rest = jnp.concatenate([low[:, whole * LANES :], high[:, whole * LANES :]], axis=1)
        out[at + 2 * whole] = rest.astype(BF16)


def unpack_pair(src, at, chans):
    whole = chans // LANES
    both = []
    for part in range(2):
        pieces = [src[at + part * whole + i].astype(F32) for i in range(whole)]
        wide = chans - whole * LANES
        if wide:
            rest = src[at + 2 * whole].astype(F32)
            pieces.append(rest[:, part * wide : (part + 1) * wide])
        both.append(jnp.concatenate(pieces, axis=1))
    return both


def single_rows(rows, chans):
    fold = -(-rows // 2 // 8) * 8
    return chans // LANES * rows + (fold if chans % LANES else 0)


def pack_single(out, value):
    rows, chans = value.shape
    whole = chans // LANES
    for i in range(whole):
        out[i * rows : (i + 1) * rows, :] = value[:, i * LANES : (i + 1) * LANES].astype(BF16)
    if chans % LANES:
        fold = -(-rows // 2 // 8) * 8
        rest = value[:, whole * LANES :]
        lower = rest[fold:]
        if 2 * fold > rows:
            blank = jnp.zeros((2 * fold - rows, chans % LANES), F32)
            lower = jnp.concatenate([lower, blank], axis=0)
        both = jnp.concatenate([rest[:fold], lower], axis=1)
        out[whole * rows : whole * rows + fold, :] = both.astype(BF16)


def unpack_single(src, rows, chans):
    whole = chans // LANES
    pieces = [src[i * rows : (i + 1) * rows, :].astype(F32) for i in range(whole)]
    wide = chans % LANES
    if wide:
        fold = -(-rows // 2 // 8) * 8
        both = src[whole * rows : whole * rows + fold, :].astype(F32)
        pieces.append(
            jnp.concatenate([both[:, :wide], both[: rows - fold, wide : 2 * wide]], axis=0)
        )
    return jnp.concatenate(pieces, axis=1)


def begin_kernel(
    carried, sent_grad, stored, image, loss_grad, gone, stored_in, image_in, loss_in, stored_out, sems
):
    rows, _, chans = stored.shape
    section = lax.axis_index("section")
    first = pltpu.make_async_copy(carried, gone, sems.at[0])
    other = pltpu.make_async_copy(sent_grad, gone, sems.at[0])
    pl.when(section == 0)(first.start)
    pl.when(section != 0)(other.start)
    copies = [
        pltpu.make_async_copy(src, dst, sems.at[1 + i])
        for i, (src, dst) in enumerate(
            ((stored, stored_in), (image, image_in), (loss_grad, loss_in))
        )
    ]
    for copy in copies:
        copy.start()
    copies[0].wait()
    step = packed_len(2, chans)
    for r in range(0, rows, 2):
        pack_pair(
            stored_out, r // 2 * step, stored_in[r].astype(F32), stored_in[r + 1].astype(F32)
        )
    for copy in copies[1:]:
        copy.wait()
    pl.when(section == 0)(first.wait)
    pl.when(section != 0)(other.wait)


def middle_kernel(
    sections, arrived, returned, image, loss_grad, stored, x_in, g_in, x_out, g_out, edges, x_edge
):
    rows, _, chans = image.shape
    section = lax.axis_index("section")
    side = lax.axis_index("band") & 1

    @pl.when(section == 0)
    def _():
        x_in[...] = image[...]

    @pl.when(section != 0)
    def _():
        x_in[...] = arrived[...]

    @pl.when(section == sections - 1)
    def _():
        g_in[...] = loss_grad[...]

    @pl.when(section != sections - 1)
    def _():
        g_in[...] = returned[...]

    row = side * (rows - 1)
    pack_pair(edges, 0, stored[row].astype(F32), g_in[row].astype(F32))
    x_edge[0] = x_in[row]
    step = packed_len(2, chans)
    for r in range(0, rows, 2):
        pack_pair(g_out, r // 2 * step, g_in[r].astype(F32), g_in[r + 1].astype(F32))
        pack_pair(x_out, r // 2 * step, x_in[r].astype(F32), x_in[r + 1].astype(F32))


def turn_kernel(kernel_t, kernel, back):
    chans = kernel.shape[1]
    for tap in range(9):
        block = kernel_t[:, tap * chans : (tap + 1) * chans]
        kernel[tap * chans : (tap + 1) * chans, :] = block.T
        back[(8 - tap) * chans : (9 - tap) * chans, :] = block


def place_of(rel, masks):
    top = max(masks).bit_length() - 1
    bits = [(rel >> i) & 1 for i in range(top + 1)]
    pos = 0
    for m in masks:
        if m & (m - 1):
            a = bits[top]
        elif m.bit_length() - 1 == top - 1:
            a = bits[top - 1] ^ bits[top]
        else:
            a = bits[m.bit_length() - 1]
        pos = pos * 2 + a
    return pos


def store_terms(terms, base, value, band, bands, masks):
    share = terms.share
    rows = value.shape[0]
    for block in range(bands):
        lo, hi = max(base, block * share), min(base + rows, (block + 1) * share)
        if lo >= hi:
            continue
        off = lo - block * share + (block * share) % 8
        pos = place_of((block ^ band) >> 1, masks)

        @pl.when((band & 1) == (block & 1))
        def _(lo=lo, hi=hi, off=off, pos=pos):
            terms.ref[pos, off : off + hi - lo, :] = value[lo - base : hi - base, :]


class Terms:
    def __init__(self, ref, share):
        self.ref = ref
        self.share = share


def send_blocks(send, blocks):
    if len(blocks) == 1:
        pack_single(send, blocks[0])
        return
    step = packed_len(2, blocks[0].shape[1])
    for i in range(0, len(blocks), 2):
        pack_pair(send, i // 2 * step, blocks[i], blocks[i + 1])


def finish_terms(terms, keep, send):
    half = keep.shape[0]
    for i in range(half):
        keep[i] = terms[i]
    send_blocks(send, [terms[half + i] for i in range(half)])


def merge_kernel(keep, got, keep_out, send_out):
    count, _, chans = keep.shape
    step = packed_len(2, chans)
    total = []
    for i in range(0, count, 2):
        low, high = unpack_pair(got, i // 2 * step, chans)
        total += [keep[i] + low, keep[i + 1] + high]
    for i in range(count // 2):
        keep_out[i] = total[i]
    send_blocks(send_out, total[count // 2 :])


def last_sum(bands, factor, keep, got, out):
    share, _, chans = out.shape
    band = lax.axis_index("band")
    starts = {b * share % 8 for b in range(bands)}
    value = (keep[0] + unpack_single(got, keep.shape[1], chans)) * factor
    for start in sorted(starts):

        @pl.when(lax.rem(band * share, 8) == start)
        def _(start=start):
            out[...] = value[start : start + share].reshape(share, 1, chans)


def load_rows(cat, own, par, side):
    rows, _, chans = own.shape
    step = packed_len(2, chans)
    for r in range(0, rows, 2):
        pair = unpack_pair(par, r // 2 * step, chans)
        for i in range(2):
            put_row(cat, 1 + rows * side + r + i, own[r + i])
            put_row(cat, 1 + rows * (1 - side) + r + i, pair[i])


def load_slab(cat, own, par, near, far, index, side):
    rows, _, chans = own.shape
    load_rows(cat, own, par, side)
    put_row(cat, (1 - side) * (2 * rows + 1), unpack_pair(near, 0, chans)[index])
    put_row(cat, side * (2 * rows + 1), unpack_pair(far, 0, chans)[index])


def back_pre(own, par, near, far, kernel, turned, slope, cat):
    rows, cols, _ = own.shape
    load_slab(cat, own, par, near, far, 0, lax.axis_index("band") & 1)
    pre = conv_rows(cat, kernel, 0, 2 * rows, cols)
    sig = jax.nn.sigmoid(pre)
    turned[...] = (pre * sig).astype(BF16).T
    slope[...] = sig * (1.0 + pre * (1.0 - sig))


def back_one(bands, masks, share, own, par, near, far, turned, cat, keep, send, terms):
    rows, cols, chans = own.shape
    band = lax.axis_index("band")
    load_slab(cat, own, par, near, far, 1, band & 1)
    held = Terms(terms, share)
    for ky in range(3):
        block = cat[(2 - ky) * cols : (2 - ky + 2 * rows) * cols, :]
        out = jnp.dot(turned[...], block, preferred_element_type=F32)
        for kx in range(3):
            store_terms(
                held,
                (3 * ky + kx) * chans,
                out[:, (2 - kx) * chans : (3 - kx) * chans],
                band,
                bands,
                masks,
            )
    finish_terms(terms, keep, send)


def back_two(
    bands, masks, share, gcat, scat, slope, kernel_t, inner, edge, keep, send, terms
):
    rows2, cols, chans = inner.shape
    band = lax.axis_index("band")
    grad = (conv_rows(gcat, kernel_t, 0, rows2, cols) * slope[...]).astype(BF16)
    inner[...] = grad.reshape(rows2, cols, chans)
    edge[0] = inner[(band & 1) * (rows2 - 1)]
    held = Terms(terms, share)
    for ky in range(3):
        out = lax.dot_general(
            scat[ky * cols : (ky + rows2) * cols, :],
            grad,
            (((0,), (0,)), ((), ())),
            preferred_element_type=F32,
        )
        store_terms(held, 3 * ky * chans, out, band, bands, masks)
    finish_terms(terms, keep, send)


def ahead_one(own, par, far, kernel, other_edge, act, edges, cat):
    rows, cols, _ = own.shape
    side = lax.axis_index("band") & 1
    load_rows(cat, own, par, side)
    put_row(cat, side * (2 * rows + 1), far[0])
    start = side * (rows - 1)
    pre = conv_rows(cat, kernel, start, rows + 1, cols)
    act[...] = (pre * jax.nn.sigmoid(pre)).astype(BF16).reshape(act.shape)
    pack_pair(edges, 0, act[side * rows].astype(F32), other_edge[0].astype(F32))


def last_conv(index, inner, edges, kernel, base, out, cat):
    rows, cols, chans = base.shape
    side = lax.axis_index("band") & 1
    for r in range(rows + 1):
        put_row(cat, 1 - side + r, inner[index * side * (rows - 1) + r])
    put_row(cat, side * (rows + 1), unpack_pair(edges, 0, chans)[index])
    total = conv_rows(cat, kernel, 0, rows, cols)
    out[...] = (base[...].astype(F32) + total.reshape(rows, cols, chans)).astype(BF16)


def body(image, carried, saved, sent_grad, loss_grad, first_kernel, second_kernel):
    rows, cols, chans = image.shape
    first, second = first_kernel[0], second_kernel[0]
    bands = lax.axis_size("band")
    sections = lax.axis_size("section")
    share = first.shape[0] // bands
    pitch = -(-(share + max(b * share % 8 for b in range(bands))) // 8) * 8
    half = bands // 2

    partner = [(b, b ^ 1) for b in range(bands)]
    beyond = [(b, b + 2 * (2 * (b & 1) - 1)) for b in range(bands)]
    beyond = [(a, b) for a, b in beyond if 0 <= b < bands]
    across = [(b, b + 2 * (b & 1) - 1) for b in range(bands)]
    across = [(a, b) for a, b in across if 0 <= b < bands]

    def move(value, pairs, axis="band"):
        return lax.ppermute(value, axis, pairs)

    whole_shape = jax.ShapeDtypeStruct(image.shape, BF16)
    row_shape = jax.ShapeDtypeStruct((1, cols, chans), BF16)

    def packed(count, rows=cols):
        return jax.ShapeDtypeStruct((packed_len(count, chans), rows, LANES), BF16)

    gone, stored, image, loss_grad, stored_out = call(
        begin_kernel,
        [whole_shape] * 4 + [packed(rows)],
        [pltpu.SemaphoreType.DMA((4,))],
        space=pltpu.HBM,
    )(*(
        pltpu.with_memory_space_constraint(v, pltpu.HBM)
        for v in (carried[0], sent_grad[0], saved[0], image, loss_grad)
    ))
    if sections == 2:
        arrived = returned = move(gone, [(0, 1), (1, 0)], "section")
    else:
        up = [(i, i + 1) for i in range(sections - 1)]
        returned = move(sent_grad[0], [(b, a) for a, b in up], "section")
        arrived = move(carried[0], up, "section")
    stored_par = move(stored_out, partner)
    x_in, g_in, x_out, g_out, edges, x_edge = call(
        functools.partial(middle_kernel, sections),
        [whole_shape, whole_shape, packed(rows), packed(rows), packed(2), row_shape],
    )(arrived, returned, image, loss_grad, stored)
    near = move(edges, beyond)
    far = move(edges, across)
    g_par = move(g_out, partner)
    x_par = move(x_out, partner)
    x_far = move(x_edge, across)

    turned_shapes = [jax.ShapeDtypeStruct(first.shape, BF16)] * 2
    first_k, first_t = call(turn_kernel, turned_shapes)(first.T)
    second_k, second_t = call(turn_kernel, turned_shapes)(second.T)

    bits = bands.bit_length() - 2
    singles = [1 << i for i in range(bits - 1)]
    last = 3 << (bits - 2)
    orders = (singles + [last], singles[::-1] + [last])

    pixels = 2 * rows * cols
    cat_shape = jax.ShapeDtypeStruct(((2 * rows + 2) * cols, 3 * chans), BF16)
    keep_shape = jax.ShapeDtypeStruct((half // 2, pitch, chans), F32)

    def send_of(count):
        if count == 1:
            return jax.ShapeDtypeStruct((single_rows(pitch, chans), LANES), BF16)
        return packed(count, pitch)

    send_shape = send_of(half // 2)
    terms = pltpu.VMEM((half, pitch, chans), F32)

    turned, slope, scat = call(
        back_pre,
        [
            jax.ShapeDtypeStruct((chans, pixels), BF16),
            jax.ShapeDtypeStruct((pixels, chans), F32),
            cat_shape,
        ],
    )(stored, stored_par, near, far, first_k)
    gcat, keep2, send2 = call(
        functools.partial(back_one, bands, orders[0], share),
        [cat_shape, keep_shape, send_shape],
        [terms],
    )(g_in, g_par, near, far, turned)
    inner, inner_edge, keep1, send1 = call(
        functools.partial(back_two, bands, orders[1], share),
        [jax.ShapeDtypeStruct((2 * rows, cols, chans), BF16), row_shape, keep_shape, send_shape],
        [terms],
    )(gcat, scat, slope, second_t)

    factor = 1.0 / math.sqrt(rows * bands * cols)

    def scatter(keep, send, masks):
        for mask in masks:
            pairs = [(b, b ^ (mask << 1)) for b in range(bands)]
            got = move(send, pairs)
            now = keep.shape[0] // 2
            if now:
                keep, send = call(
                    merge_kernel,
                    [jax.ShapeDtypeStruct((now, pitch, chans), F32), send_of(now)],
                )(keep, got)
        return call(
            functools.partial(last_sum, bands, factor),
            jax.ShapeDtypeStruct((share, 1, chans), F32),
        )(keep, got).reshape(1, share, chans)

    second_sum = scatter(keep2, send2, orders[0])
    first_sum = scatter(keep1, send1, orders[1])

    small_cat = pltpu.VMEM(((rows + 2) * cols, 3 * chans), BF16)
    act, edges = call(
        ahead_one,
        [jax.ShapeDtypeStruct((rows + 1, cols, chans), BF16), packed(2)],
        [pltpu.VMEM(cat_shape.shape, BF16)],
    )(x_in, x_par, x_far, first_k, inner_edge)
    edges = move(edges, across)
    forward_out = call(
        functools.partial(last_conv, 0),
        jax.ShapeDtypeStruct(x_in.shape, BF16),
        [small_cat],
    )(act, edges, second_k, x_in)
    input_grad = call(
        functools.partial(last_conv, 1),
        jax.ShapeDtypeStruct(g_in.shape, BF16),
        [small_cat],
    )(inner, edges, first_t, g_in)
    return (
        forward_out[None],
        input_grad[None],
        first_sum,
        second_sum,
    )


def solution(mesh):
    return jax.shard_map(
        body,
        mesh=mesh,
        in_specs=(
            P("band", None, None),
            P("section", "band", None, None),
            P("section", "band", None, None),
            P("section", "band", None, None),
            P("band", None, None),
            P("section", None, None),
            P("section", None, None),
        ),
        out_specs=(
            P("section", "band", None, None),
            P("section", "band", None, None),
            P("section", "band", None),
            P("section", "band", None),
        ),
        check_vma=False,
    )
```
